32 devices in a mesh: mode: 8 (over z, y), gz: 4 (over x, core).
Axes of the slice: x: 2, y: 2, z: 4, core: 2. Of those that a mesh axis runs over, the one named last changes fastest.
Arguments:
- efield: float32 [3, 256, 64, 256], P(None, 'mode', 'gz'), may hold values from -0.6 to 0.6
- hfield: float32 [3, 256, 64, 256], P(None, 'mode', 'gz'), may hold values from -0.6 to 0.6
- polar: float32 [3, 4, 16, 256, 512], P(None, 'gz', 'mode'), may hold values from -1.2 to 1.2
- velocity: float32 [3, 4, 16, 256, 512], P(None, 'gz', 'mode'), may hold values from -0.5 to 0.5
- material: float32 [4, 4, 16, 256], P(None, 'gz', 'mode'), may hold values from 0.05 to 0.5
Outputs:
- new_efield: float32 [3, 256, 64, 256], P(None, 'mode', 'gz')
- new_hfield: float32 [3, 256, 64, 256], P(None, 'mode', 'gz')
- new_polar: float32 [3, 4, 16, 256, 512], P(None, 'gz', 'mode')
- new_velocity: float32 [3, 4, 16, 256, 512], P(None, 'gz', 'mode')
The draws below stay inside these ranges and needn't reach their ends.
All inputs are finite; a program needn't handle non-finite values.
Results may differ from the reference program's by a relative error of at most 0.0001.
Values sent between devices are 32-bit elements; how exact they have to be, the bound alone decides.
No kernel may reach another device: no remote copies, remote signals or barrier semaphores. Data moves between devices by JAX's collectives and lax.ppermute only.
A program may use at most 64 MiB of HBM per device.

```python
import math
import jax
import jax.numpy as jnp
from jax import lax

M = 256
R = 256
NA = 512
Z_DEV = 16
STEPS = 2
SUBSTEPS = 4
NZ = 64
N_GZ = 4


def level_of(stream_key, shape, split, low, top_value):
    gain = 1.0
    for position, blocks in split:
        draws = jax.random.uniform(jax.random.fold_in(jax.random.fold_in(stream_key, 6), position), (blocks,), jnp.float32, low / len(split), top_value / len(split))
        gain = gain * jnp.repeat(jnp.exp(draws), shape[position] // blocks).reshape((-1,) + (1,) * (len(shape) - 1 - position))
    return gain


def gaussian(stream_key, dims, spread, reach, split=(), held_as=jnp.bfloat16):
    result = spread * jax.random.normal(stream_key, dims, jnp.float32)
    if split:
        result = result * level_of(stream_key, dims, split, -0.22, 0.18)
    return jnp.clip(result, -reach, reach).astype(held_as)


def setup_inputs(seed: int = 0) -> dict:
    seeds = jax.random.split(jax.random.key(seed), 6)
    efield = gaussian(seeds[0], (3, M, NZ, R), 0.1, 0.6, ((1, 8), (2, 4)), jnp.float32)
    hfield = gaussian(seeds[1], (3, M, NZ, R), 0.1, 0.6, ((1, 8), (2, 4)), jnp.float32)
    polar = gaussian(seeds[2], (3, N_GZ, Z_DEV, R, NA), 0.4, 1.2, ((1, 4), (2, 8)), jnp.float32)
    velocity = gaussian(seeds[3], (3, N_GZ, Z_DEV, R, NA), 0.1, 0.5, ((1, 4), (2, 8)), jnp.float32)
    material = jnp.clip(jnp.exp(math.log(0.5) - 2.3025851 * jax.random.uniform(seeds[4], (4, N_GZ, Z_DEV, R), jnp.float32) ** level_of(seeds[4], (4, N_GZ, Z_DEV, R), ((1, 4), (2, 8)), -0.2, 0.2)), 0.05, 0.5)
    return dict(efield=efield, hfield=hfield, polar=polar, velocity=velocity, material=material)


axial_ratio = 0.5
highest = lax.Precision.HIGHEST


def tables():
    order = jnp.arange(M, dtype=jnp.int32) // 2
    parity = jnp.arange(M, dtype=jnp.int32) % 2
    angles = jnp.arange(NA, dtype=jnp.int32)
    phase = (order[:, None] * angles[None, :]) % NA
    theta = phase.astype(jnp.float32) * (2.0 * math.pi / NA)
    basis = jnp.where(parity[:, None] == 0, jnp.cos(theta), jnp.sin(theta))
    weights = jnp.where(jnp.arange(M, dtype=jnp.int32) == 0, 1.0 / NA, 2.0 / NA).astype(jnp.float32)
    return basis, basis * weights[:, None]


def azimuthal(field, orders):
    count, planes, radii = field.shape
    pairs = field.reshape(count // 2, 2, planes, radii)
    scale = orders.astype(jnp.float32)[:, None, None]
    return jnp.stack([scale * pairs[:, 1], -scale * pairs[:, 0]], axis=1).reshape(field.shape)


def radial_down(field):
    return field - jnp.concatenate([jnp.zeros_like(field[..., :1]), field[..., :-1]], axis=-1)


def radial_up(field):
    return jnp.concatenate([field[..., 1:], jnp.zeros_like(field[..., :1])], axis=-1) - field


def axial_up(field, above):
    return jnp.concatenate([field[:, 1:], above[:, None]], axis=1) - field


def axial_down(field, below):
    return field - jnp.concatenate([below[:, None], field[:, :-1]], axis=1)


def update_magnetic(efield, hfield, above, orders):
    time_step = 0.7 / M
    outer = jnp.arange(R, dtype=jnp.float32) + 1.0
    inner = jnp.arange(R, dtype=jnp.float32) + 0.5
    h_radial = hfield[0] - time_step * azimuthal(efield[2], orders) / outer + axial_ratio * axial_up(efield[1], above[1])
    h_azimuth = hfield[1] - axial_ratio * axial_up(efield[0], above[0]) + time_step * radial_down(efield[2])
    h_axial = hfield[2] - time_step * (radial_down(outer * efield[1]) - azimuthal(efield[0], orders)) / inner
    return jnp.stack([h_radial, h_azimuth, h_axial])


def update_electric(efield, hfield, below, orders, change):
    time_step = 0.7 / M
    outer = jnp.arange(R, dtype=jnp.float32) + 1.0
    inner = jnp.arange(R, dtype=jnp.float32) + 0.5
    e_radial = efield[0] + time_step * azimuthal(hfield[2], orders) / inner - axial_ratio * axial_down(hfield[1], below[1]) - change[0]
    e_azimuth = efield[1] + axial_ratio * axial_down(hfield[0], below[0]) - time_step * radial_up(hfield[2]) - change[1]
    e_axial = efield[2] + time_step * (radial_up(inner * hfield[1]) - azimuthal(hfield[0], orders)) / outer - change[2]
    return jnp.stack([e_radial, e_azimuth, e_axial])


def respond(points, polar, velocity, material):
    stiff = material[0][..., None]
    damping = material[1][..., None]
    couple = material[2][..., None]
    harden = 0.1 * material[3][..., None]
    before = polar
    for substep in range(SUBSTEPS):
        energy = jnp.sum(polar * polar, axis=0, keepdims=True)
        drive = stiff * (couple * points - polar) - harden * energy * polar
        velocity = ((1.0 - 0.5 * damping) * velocity + drive) / (1.0 + 0.5 * damping)
        polar = polar + velocity
    return polar, velocity, polar - before


def reference(efield, hfield, polar, velocity, material):
    basis, project = tables()
    orders = jnp.arange(M // 2, dtype=jnp.int32)
    edge = jnp.zeros((2, M, R), jnp.float32)
    polar_planes = jnp.transpose(polar.reshape(3, NZ, R, NA), (1, 0, 2, 3))
    velocity_planes = jnp.transpose(velocity.reshape(3, NZ, R, NA), (1, 0, 2, 3))
    material_planes = jnp.transpose(material.reshape(4, NZ, R), (1, 0, 2))

    def plane(operands):
        e_plane, p_plane, v_plane, m_plane = operands
        points = jnp.einsum("ckr,kn->crn", e_plane, basis, precision=highest)
        p_next, v_next, change = respond(points, p_plane, v_plane, m_plane)
        modal = jnp.einsum("crn,kn->ckr", change, project, precision=highest)
        return p_next, v_next, modal

    for step in range(STEPS):
        e_planes = jnp.transpose(efield, (2, 0, 1, 3))
        hfield = update_magnetic(efield, hfield, edge, orders)
        polar_planes, velocity_planes, modal = lax.map(plane, (e_planes, polar_planes, velocity_planes, material_planes))
        change = jnp.transpose(modal, (1, 2, 0, 3))
        efield = update_electric(efield, hfield, edge, orders, change)
    new_polar = jnp.transpose(polar_planes, (1, 0, 2, 3)).reshape(3, N_GZ, Z_DEV, R, NA)
    new_velocity = jnp.transpose(velocity_planes, (1, 0, 2, 3)).reshape(3, N_GZ, Z_DEV, R, NA)
    return efield, hfield, new_polar, new_velocity
```

```python
import functools
import math

import jax
import jax.numpy as jnp
from jax import lax
from jax.experimental import pallas as pl
from jax.experimental.pallas import tpu as pltpu
from jax.sharding import PartitionSpec as P

SUBSTEPS = 4
LANES = 128
RATIO = 0.5


def tables(modes, angles):
    order = jnp.arange(modes, dtype=jnp.int32) // 2
    parity = jnp.arange(modes, dtype=jnp.int32) % 2
    steps = jnp.arange(angles, dtype=jnp.int32)
    phase = order[:, None] * steps[None, :] % angles
    theta = phase.astype(jnp.float32) * (2.0 * math.pi / angles)
    return jnp.where(parity[:, None] == 0, jnp.cos(theta), jnp.sin(theta))


def split(value):
    high = value.astype(jnp.bfloat16)
    return high, (value - high.astype(jnp.float32)).astype(jnp.bfloat16)


class Plane:
    def __init__(self, first, modes, radii, total):
        row = lax.broadcasted_iota(jnp.int32, (modes, radii), 0)
        self.lane = lax.broadcasted_iota(jnp.int32, (modes, radii), 1)
        self.even = row % 2 == 0
        order = ((first + row) // 2).astype(jnp.float32)
        self.signed = jnp.where(self.even, order, -order)
        self.modes, self.radii = modes, radii
        self.time_step = 0.7 / total
        place = self.lane.astype(jnp.float32)
        self.outer = place + 1.0
        self.inner = place + 0.5
        self.per_outer = 1.0 / self.outer
        self.per_inner = 1.0 / self.inner

    def rotate(self, x):
        swapped = jnp.where(
            self.even, pltpu.roll(x, self.modes - 1, 0), pltpu.roll(x, 1, 0)
        )
        return self.signed * swapped

    def down(self, x):
        return x - jnp.where(self.lane == 0, 0.0, pltpu.roll(x, 1, 1))

    def up(self, x):
        return jnp.where(self.lane == self.radii - 1, 0.0, pltpu.roll(x, self.radii - 1, 1)) - x

    def magnetic(self, e, e_above, h):
        ts = self.time_step
        return (
            h[0] - (ts * self.per_outer) * self.rotate(e[2]) + RATIO * (e_above[1] - e[1]),
            h[1] - RATIO * (e_above[0] - e[0]) + ts * self.down(e[2]),
            h[2] - (ts * self.per_inner) * (self.down(self.outer * e[1]) - self.rotate(e[0])),
        )

    def curl(self, h, h_below):
        ts = self.time_step
        return (
            (ts * self.per_inner) * self.rotate(h[2]) - RATIO * (h[1] - h_below[1]),
            RATIO * (h[0] - h_below[0]) - ts * self.up(h[2]),
            (ts * self.per_outer) * (self.up(self.inner * h[1]) - self.rotate(h[0])),
        )


def to_zk(source, target):
    count, modes, planes, _ = source.shape
    for c in range(count):
        for k in range(0, modes, 8):
            for z in range(0, planes, 8):
                target[c, z : z + 8, k : k + 8, :] = jnp.swapaxes(
                    source[c, k : k + 8, z : z + 8, :], 0, 1
                )


def to_kz(source, target):
    count, planes, modes, _ = source.shape
    for c in range(count):
        for k in range(0, modes, 8):
            for z in range(0, planes, 8):
                target[c, k : k + 8, z : z + 8, :] = jnp.swapaxes(
                    source[c, z : z + 8, k : k + 8, :], 0, 1
                )


def pack_kernel(place, e_kz, h_edge, *outs):
    blocks, (e_zk, to_lower, to_upper) = outs[:-3], outs[-3:]
    peers = len(blocks)
    me = place[0]
    to_zk(e_kz, e_zk)
    planes = e_zk.shape[1] // peers
    last = e_zk.shape[1] - 1
    for s in reversed(range(peers)):
        first = (me ^ s) * planes
        for c in range(3):
            for q in range(planes):
                blocks[s][c * planes + q] = e_zk[c, first + q]
    for c in range(2):
        to_lower[c] = e_zk[c, 0]
    for c in range(3):
        to_upper[c] = e_zk[c, last]
    for c in range(2):
        to_upper[3 + c] = h_edge[c, :, h_edge.shape[2] - 1, :]


def unpack_kernel(place, ahead, h_zk, *refs):
    blocks, (e_zk, to_lower, to_upper) = refs[:-3], refs[-3:]
    peers = len(blocks)
    me = place[0]
    planes = e_zk.shape[1] // peers
    last = e_zk.shape[1] - 1
    for s in range(peers):
        first = (me ^ s) * planes
        for c in range(2):
            for q in range(planes):
                e_zk[c, first + q] = ahead[c, first + q] - blocks[s][c * planes + q]
        for q in range(planes - 1):
            e_zk[2, first + q] = ahead[2, first + q]
        e_zk[2, first + planes - 1] = ahead[2, first + planes - 1] - blocks[s][2 * planes]
    for c in range(2):
        to_lower[c] = e_zk[c, 0]
    for c in range(3):
        to_upper[c] = e_zk[c, last]
    for c in range(2):
        to_upper[3 + c] = h_zk[c, last]


def advance(place, e, base, h, above, below, h_new, store):
    planes, modes, radii = e.shape[1:]
    op = Plane(place[0] * modes, modes, radii, place_total(modes, place))
    def magnetic(z, e_above):
        new = op.magnetic([e[c, z] for c in range(3)], e_above, [h[c, z] for c in range(3)])
        for c in range(3):
            h_new[c, z] = new[c]

    def loop_h(z, carry):
        magnetic(z, [e[c, z + 1] for c in range(2)])
        return carry

    lax.fori_loop(0, planes - 1, loop_h, 0)
    magnetic(planes - 1, [above[c] for c in range(2)])
    edge = op.magnetic(
        [below[c] for c in range(3)], [e[c, 0] for c in range(2)], [below[3], below[4], below[4]]
    )
    inside = place[1] > 0
    edge = [jnp.where(inside, edge[c], 0.0) for c in range(2)]

    def electric(z, h_below):
        curl = op.curl([h_new[c, z] for c in range(3)], h_below)
        store(z, curl, [base[c, z] for c in range(3)])

    electric(0, edge)

    def loop_e(z, carry):
        electric(z, [h_new[c, z - 1] for c in range(2)])
        return carry

    lax.fori_loop(1, planes, loop_e, 0)


def place_total(modes, place):
    return modes * PEERS[0]


PEERS = [0]


def first_kernel(place, e_zk, h_kz, above, below, *refs):
    h_zk, curl = refs[-2:]
    blocks, (ahead, h_new) = refs[:-4], refs[-4:-2]
    peers = len(blocks)
    me = place[0]
    to_zk(h_kz, h_zk)

    def store(z, found, base):
        for c in range(3):
            curl[c, z] = found[c]
            ahead[c, z] = base[c] + found[c]

    advance(place, e_zk, e_zk, h_zk, above, below, h_new, store)
    planes = e_zk.shape[1] // peers
    for s in reversed(range(peers)):
        first = (me ^ s) * planes
        for c in range(2):
            for q in range(planes):
                blocks[s][c * planes + q] = curl[c, first + q]
        blocks[s][2 * planes] = curl[2, first]


def last_kernel(place, e_zk, ahead, h_zk, above, below, ahead_new, h_kz, h_new):
    def store(z, found, base):
        for c in range(3):
            ahead_new[c, z] = base[c] + found[c]

    advance(place, e_zk, ahead, h_zk, above, below, h_new, store)
    to_kz(h_new, h_kz)


def finish_kernel(place, ahead, *refs):
    blocks, (e_kz, e_zk) = refs[:-2], refs[-2:]
    peers = len(blocks)
    planes = e_zk.shape[1] // peers
    for s in range(peers):
        first = (place[0] ^ s) * planes
        for c in range(3):
            for q in range(planes):
                e_zk[c, first + q] = ahead[c, first + q] - blocks[s][c * planes + q]
    to_kz(e_zk, e_kz)


def respond(table, fields, points, polar, velocity, coefficient, new_polar, new_velocity, store):
    high, low = table
    rows, angles = polar.shape[-2:]
    for c in range(3):
        f_high, f_low = split(fields(c).T)
        points[c] = (
            jnp.dot(f_high, high[...], preferred_element_type=jnp.float32)
            + jnp.dot(f_high, low[...], preferred_element_type=jnp.float32)
            + jnp.dot(f_low, high[...], preferred_element_type=jnp.float32)
        )
    width = min(angles, 256)

    def loop(g, carry):
        at = pl.ds(pl.multiple_of(g * 8, 8), 8)
        keep, push, spring, hard = [
            jnp.broadcast_to(coefficient[0, at, n : n + 1], (8, width)) for n in range(4)
        ]
        for start in range(0, angles, width):
            part = slice(start, start + width)
            before = [polar[c, 0, 0, at, part] for c in range(3)]
            v = [velocity[c, 0, 0, at, part] for c in range(3)]
            drive = [push * points[c, at, part] for c in range(3)]
            p = before
            for substep in range(SUBSTEPS):
                energy = p[0] * p[0] + p[1] * p[1] + p[2] * p[2]
                pull = spring + hard * energy
                v = [keep * v[c] + (drive[c] - pull * p[c]) for c in range(3)]
                p = [p[c] + v[c] for c in range(3)]
            for c in range(3):
                new_polar[c, 0, 0, at, part] = p[c]
                new_velocity[c, 0, 0, at, part] = v[c]
                points[c, at, part] = p[c] - before[c]
        return carry

    lax.fori_loop(0, rows // 8, loop, 0)
    modes = high.shape[0]
    weight = jnp.where(
        lax.broadcasted_iota(jnp.int32, (modes, rows), 0) == 0, 1.0 / angles, 2.0 / angles
    )
    contract = (((1,), (1,)), ((), ()))
    for c in range(3):
        c_high, c_low = split(points[c])
        modal = (
            lax.dot_general(high[...], c_high, contract, preferred_element_type=jnp.float32)
            + lax.dot_general(low[...], c_high, contract, preferred_element_type=jnp.float32)
            + lax.dot_general(high[...], c_low, contract, preferred_element_type=jnp.float32)
        )
        store(c, weight * modal)


def gas_step(basis, fields, points, high, low, polar, velocity, coefficient, new_polar, new_velocity, change):
    q, part = pl.program_id(0), pl.program_id(1)
    planes = pl.num_programs(0)
    rows = polar.shape[-2]
    at = pl.ds(pl.multiple_of(part * rows, rows), rows)

    def store(c, modal):
        change[c * planes + q, :, at] = modal

    respond(
        (high, low), lambda c: fields[c * planes + q, :, at], points,
        polar, velocity, coefficient, new_polar, new_velocity, store,
    )


def is_first():
    return jnp.logical_and(pl.program_id(0) == 0, pl.program_id(1) == 0)


def is_last():
    return jnp.logical_and(
        pl.program_id(0) == pl.num_programs(0) - 1, pl.program_id(1) == pl.num_programs(1) - 1
    )


def gas_first_kernel(peers, planes, place, basis, coefficient, polar, velocity, *refs):
    arrived, refs = refs[:peers], refs[peers:]
    blocks, refs = refs[:peers], refs[peers:]
    new_polar, new_velocity, change, rest, fields, points, high, low = refs
    me = place[0]
    modes, radii = arrived[0].shape[1:]

    @pl.when(is_first())
    def _():
        high[...], low[...] = split(basis[...])
        for s in range(peers):
            at = pl.ds(pl.multiple_of((me ^ s) * modes, modes), modes)
            for n in range(3 * planes):
                fields[n, at, :] = arrived[s][n]

    gas_step(basis, fields, points, high, low, polar, velocity, coefficient, new_polar, new_velocity, change)

    @pl.when(is_last())
    def _():
        for s in range(peers):
            first = (me ^ s) * modes
            at = pl.ds(pl.multiple_of(first, modes), modes)
            op = Plane(first, modes, radii, modes * peers)
            for n in range(3 * planes):
                rest[n, at, :] = fields[n, at, :] - change[n, at, :]
            phi, axial = None, change[2 * planes, at, :]
            for q in range(planes):
                for c in range(2):
                    sent = change[c * planes + q, at, :]
                    if phi is not None:
                        sent = sent + (op.down(phi) if c == 0 else op.per_outer * op.rotate(phi))
                    blocks[s][c * planes + q] = sent
                if q < planes - 1:
                    phi = (-op.time_step / RATIO) * axial
                    axial = axial + change[2 * planes + q + 1, at, :]
            blocks[s][2 * planes] = axial


def gas_last_kernel(peers, planes, place, basis, coefficient, polar, velocity, rest, earlier, *refs):
    arrived, refs = refs[:peers], refs[peers:]
    blocks, refs = refs[:peers], refs[peers:]
    new_polar, new_velocity, fields, points, high, low, change = refs
    me = place[0]
    modes, radii = arrived[0].shape[1:]

    @pl.when(is_first())
    def _():
        high[...], low[...] = split(basis[...])
        for s in range(peers):
            first = (me ^ s) * modes
            at = pl.ds(pl.multiple_of(first, modes), modes)
            op = Plane(first, modes, radii, modes * peers)
            axial = arrived[s][2 * planes]
            for q in range(planes):
                radial, azimuth = arrived[s][q], arrived[s][planes + q]
                if q > 0:
                    flux = op.up(op.inner * radial) + op.rotate(azimuth)
                    axial = axial - (op.time_step / RATIO) * op.per_outer * flux
                for c, found in enumerate((radial, azimuth, axial)):
                    n = c * planes + q
                    fields[n, at, :] = rest[n, at, :] + found

    gas_step(basis, fields, points, high, low, polar, velocity, coefficient, new_polar, new_velocity, change)

    @pl.when(is_last())
    def _():
        for s in reversed(range(peers)):
            at = pl.ds(pl.multiple_of((me ^ s) * modes, modes), modes)
            for n in range(3 * planes):
                blocks[s][n] = earlier[n, at, :] + change[n, at, :]


def f32(*shape):
    return jax.ShapeDtypeStruct(shape, jnp.float32)


def call(kernel, name, out, place, *operands, scratch=(), flops=0):
    moved = sum(4 * math.prod(x.shape) for x in (*operands, *out))
    whole = [pl.BlockSpec(memory_space=pltpu.VMEM)] * len(operands)
    return pl.pallas_call(
        kernel,
        name=name,
        out_shape=out,
        in_specs=[pl.BlockSpec(memory_space=pltpu.SMEM)] + whole,
        out_specs=[pl.BlockSpec(memory_space=pltpu.VMEM)] * len(out),
        scratch_shapes=[pltpu.VMEM(shape, jnp.float32) for shape in scratch],
        cost_estimate=pl.CostEstimate(flops=flops, bytes_accessed=moved, transcendentals=0),
    )(place, *operands)


def gas_call(kernel, name, place, basis, coefficient, polar, velocity, extra, arrived, blocks, kept, planes):
    peers = len(arrived)
    modes, angles = basis.shape
    radii = polar.shape[3]
    rows = min(radii, LANES)
    whole = lambda x: pl.BlockSpec(x.shape, lambda q, r, n=len(x.shape): (0,) * n)
    state = pl.BlockSpec((3, 1, 1, rows, angles), lambda q, r: (0, 0, q, r, 0))
    local = pl.BlockSpec((1, rows, coefficient.shape[2]), lambda q, r: (q, r, 0))
    out = [*blocks, f32(*polar.shape), f32(*velocity.shape), *kept]
    scratch = [
        pltpu.VMEM((3 * planes, modes, radii), jnp.float32),
        pltpu.VMEM((3, rows, angles), jnp.float32),
        pltpu.VMEM((modes, angles), jnp.bfloat16),
        pltpu.VMEM((modes, angles), jnp.bfloat16),
    ]
    if not kept:
        scratch.append(pltpu.VMEM((3 * planes, modes, radii), jnp.float32))
    moved = sum(4 * math.prod(x.shape) for x in (*out, polar, velocity, *extra, *arrived))
    return pl.pallas_call(
        functools.partial(kernel, peers, planes),
        name=name,
        grid=(planes, radii // rows),
        out_shape=out,
        in_specs=[
            pl.BlockSpec(memory_space=pltpu.SMEM), whole(basis), local, state, state,
            *[whole(x) for x in (*extra, *arrived)],
        ],
        out_specs=[*[whole(x) for x in blocks], state, state, *[whole(x) for x in kept]],
        scratch_shapes=scratch,
        cost_estimate=pl.CostEstimate(
            flops=12 * 3 * planes * radii * modes * angles, bytes_accessed=moved, transcendentals=0
        ),
    )(place, basis, coefficient, polar, velocity, *extra, *arrived)


def exchange(blocks):
    peers = len(blocks)
    moved = [None] * peers
    moved[0] = blocks[0]
    for s in reversed(range(1, peers)):
        moved[s] = lax.ppermute(blocks[s], "mode", [(i, i ^ s) for i in range(peers)])
    return moved


def along(value, steps):
    count = lax.axis_size("gz")
    first, last = max(0, -steps), min(count, count - steps)
    return lax.ppermute(value, "gz", [(i, i + steps) for i in range(first, last)])


def on_device(efield, hfield, polar, velocity, material):
    peers = lax.axis_size("mode")
    PEERS[0] = peers
    _, modes, depth, radii = efield.shape
    planes = depth // peers
    angles = polar.shape[4]
    place = jnp.stack([lax.axis_index("mode"), lax.axis_index("gz")]).astype(jnp.int32)
    electric = [f32(3 * planes, modes, radii)] * peers
    curled = [f32(2 * planes + 1, modes, radii)] * peers
    zk = f32(3, depth, modes, radii)
    kz = f32(3, modes, depth, radii)
    lower, upper = f32(2, modes, radii), f32(5, modes, radii)

    h_edge = hfield[0:2, :, depth - 1 :, :]
    *blocks, e_zk, to_lower, to_upper = call(
        pack_kernel, "pack", [*electric, zk, lower, upper], place, efield, h_edge
    )
    arrived = exchange(blocks)
    above, below = along(to_lower, -1), along(to_upper, 1)

    stiff, damp, couple, harden = [material[n, 0] for n in range(4)]
    scale = 1.0 / (1.0 + 0.5 * damp)
    coefficient = jnp.stack(
        [(1.0 - 0.5 * damp) * scale, stiff * couple * scale, stiff * scale, 0.1 * harden * scale], axis=-1
    )
    basis = tables(modes * peers, angles)

    *curl_blocks, ahead, h_zk = call(
        first_kernel, "first", [*curled, zk, zk], place, e_zk, hfield, above, below,
        scratch=[zk.shape, zk.shape],
    )
    curl_arrived = exchange(curl_blocks)

    held = f32(3 * planes, modes * peers, radii)
    *back, polar, velocity, change, rest = gas_call(
        gas_first_kernel, "gas_first", place, basis, coefficient, polar, velocity,
        [], arrived, curled, [held, held], planes,
    )
    returned = exchange(back)
    *back, polar, velocity = gas_call(
        gas_last_kernel, "gas_last", place, basis, coefficient, polar, velocity,
        [rest, change], curl_arrived, electric, [], planes,
    )
    total = exchange(back)

    e_zk, to_lower, to_upper = call(
        unpack_kernel, "unpack", [zk, lower, upper], place, ahead, h_zk, *returned
    )
    above, below = along(to_lower, -1), along(to_upper, 1)
    ahead, new_hfield = call(
        last_kernel, "last", [zk, kz], place, e_zk, ahead, h_zk, above, below, scratch=[zk.shape]
    )
    (new_efield,) = call(finish_kernel, "finish", [kz], place, ahead, *total, scratch=[zk.shape])
    return new_efield, new_hfield, polar, velocity


def solution(mesh):
    field = P(None, "mode", "gz", None)
    state = P(None, "gz", "mode", None, None)
    return jax.shard_map(
        on_device,
        mesh=mesh,
        in_specs=(field, field, state, state, P(None, "gz", "mode", None)),
        out_specs=(field, field, state, state),
        check_vma=False,
    )
```

```python
import functools
import math

import jax
import jax.numpy as jnp
from jax import lax
from jax.experimental import pallas as pl
from jax.experimental.pallas import tpu as pltpu
from jax.sharding import PartitionSpec as P


SUBSTEPS = 4
LANES = 128
RATIO = 0.5


def distances(peers):
    quarter = peers // 4
    far, near = list(range(3 * quarter, peers)), list(range(1, quarter))
    middle = list(range(3 * quarter - 1, quarter - 1, -1))
    far.reverse()
    inner, outer = far[:1] + far[1:] + near, near[:1] + far[1:] + far[:1] + near[1:]
    return inner + middle + [0], outer + middle + [0]


def peer(me, s, peers):
    inner, outer = (by_class[s] for by_class in distances(peers))
    if inner == outer:
        return me ^ inner
    return me ^ jnp.where(is_inner(me, peers), inner, outer)


def is_inner(me, peers):
    quarter = peers // 4
    return (me >= quarter) & (me < 3 * quarter)


def tables(modes, angles):
    order = jnp.arange(modes, dtype=jnp.int32) // 2
    parity = jnp.arange(modes, dtype=jnp.int32) % 2
    steps = jnp.arange(angles, dtype=jnp.int32)
    phase = order[:, None] * steps[None, :] % angles
    theta = phase.astype(jnp.float32) * (2.0 * math.pi / angles)
    return jnp.where(parity[:, None] == 0, jnp.cos(theta), jnp.sin(theta))


def split(value):
    high = value.astype(jnp.bfloat16)
    return high, (value - high.astype(jnp.float32)).astype(jnp.bfloat16)


class Plane:
    def __init__(self, first, modes, radii, total):
        row = lax.broadcasted_iota(jnp.int32, (modes, radii), 0)
        self.lane = lax.broadcasted_iota(jnp.int32, (modes, radii), 1)
        self.even = row % 2 == 0
        order = ((first + row) // 2).astype(jnp.float32)
        self.signed = jnp.where(self.even, order, -order)
        self.modes, self.radii = modes, radii
        self.time_step = 0.7 / total
        place = self.lane.astype(jnp.float32)
        self.outer = place + 1.0
        self.inner = place + 0.5
        self.per_outer = 1.0 / self.outer
        self.per_inner = 1.0 / self.inner

    def rotate(self, x):
        swapped = jnp.where(
            self.even, pltpu.roll(x, self.modes - 1, 0), pltpu.roll(x, 1, 0)
        )
        return self.signed * swapped

    def down(self, x):
        return x - jnp.where(self.lane == 0, 0.0, pltpu.roll(x, 1, 1))

    def up(self, x):
        return jnp.where(self.lane == self.radii - 1, 0.0, pltpu.roll(x, self.radii - 1, 1)) - x

    def magnetic(self, e, e_above, h):
        ts = self.time_step
        return (
            h[0] - (ts * self.per_outer) * self.rotate(e[2]) + RATIO * (e_above[1] - e[1]),
            h[1] - RATIO * (e_above[0] - e[0]) + ts * self.down(e[2]),
            h[2] - (ts * self.per_inner) * (self.down(self.outer * e[1]) - self.rotate(e[0])),
        )

    def curl(self, h, h_below):
        ts = self.time_step
        return (
            (ts * self.per_inner) * self.rotate(h[2]) - RATIO * (h[1] - h_below[1]),
            RATIO * (h[0] - h_below[0]) - ts * self.up(h[2]),
            (ts * self.per_outer) * (self.up(self.inner * h[1]) - self.rotate(h[0])),
        )


def to_zk(source, target):
    count, modes, planes, _ = source.shape
    for c in range(count):
        for k in range(0, modes, 8):
            for z in range(0, planes, 8):
                target[c, z : z + 8, k : k + 8, :] = jnp.swapaxes(
                    source[c, k : k + 8, z : z + 8, :], 0, 1
                )


def to_kz(source, target):
    count, planes, modes, _ = source.shape
    for c in range(count):
        for k in range(0, modes, 8):
            for z in range(0, planes, 8):
                target[c, k : k + 8, z : z + 8, :] = jnp.swapaxes(
                    source[c, z : z + 8, k : k + 8, :], 0, 1
                )


def pack_kernel(e_kz, h_kz, *refs):
    outs, (held, e_zk, tail, h_last, in_sem, out_sem, edge_sem) = refs[:-7], refs[-7:]
    blocks, (to_lower, to_upper) = outs[:-2], outs[-2:]
    peers = len(blocks)
    depth = e_zk.shape[1]
    planes = depth // peers
    me = lax.axis_index("mode")
    loads = [pltpu.make_async_copy(e_kz.at[c], held.at[c], in_sem.at[c]) for c in range(3)]
    loads.append(pltpu.make_async_copy(h_kz.at[:, :, pl.ds(depth - 8, 8)], tail, in_sem.at[3]))
    for load in loads:
        load.start()
    stores = []

    def store(source, target, semaphore):
        stores.append(pltpu.make_async_copy(source, target, semaphore))
        stores[-1].start()

    for c in range(3):
        loads[c].wait()
        to_zk(held.at[pl.ds(c, 1)], e_zk.at[pl.ds(c, 1)])
        for s in range(peers):
            first = peer(me, s, peers) * planes
            store(
                e_zk.at[c, pl.ds(first, planes)], blocks[s].at[pl.ds(c * planes, planes)], out_sem.at[c, s]
            )
    store(e_zk.at[:, 0], to_lower, edge_sem.at[0])
    store(e_zk.at[:, depth - 1], to_upper.at[0], edge_sem.at[1])
    loads[3].wait()
    for c in range(3):
        h_last[c] = tail[c, :, 7, :]
    store(h_last, to_upper.at[1], edge_sem.at[2])
    for copy in stores:
        copy.wait()


def unpack_kernel(ahead, h_zk, *refs):
    blocks, (e_zk, to_lower, to_upper) = refs[:-3], refs[-3:]
    peers = len(blocks)
    me = lax.axis_index("mode")
    planes = e_zk.shape[1] // peers
    last = e_zk.shape[1] - 1
    for s in range(peers):
        first = peer(me, s, peers) * planes
        for c in range(2):
            for q in range(planes):
                e_zk[c, first + q] = ahead[c, first + q] - blocks[s][c * planes + q]
        for q in range(planes - 1):
            e_zk[2, first + q] = ahead[2, first + q]
        e_zk[2, first + planes - 1] = ahead[2, first + planes - 1] - blocks[s][2 * planes]
    for c in range(3):
        to_lower[c] = e_zk[c, 0]
        to_upper[0, c] = e_zk[c, last]
        to_upper[1, c] = h_zk[c, last]


def advance(peers, e, base, h, above, below, h_new, store):
    planes, modes, radii = e.shape[1:]
    op = Plane(lax.axis_index("mode") * modes, modes, radii, modes * peers)

    def magnetic(z, e_above):
        new = op.magnetic([e[c, z] for c in range(3)], e_above, [h[c, z] for c in range(3)])
        for c in range(3):
            h_new[c, z] = new[c]

    def loop_h(z, carry):
        magnetic(z, [e[c, z + 1] for c in range(2)])
        return carry

    lax.fori_loop(0, planes - 1, loop_h, 0)
    magnetic(planes - 1, [above[c] for c in range(2)])
    edge = op.magnetic(
        [below[0, c] for c in range(3)], [e[c, 0] for c in range(2)], [below[1, c] for c in range(3)]
    )
    inside = lax.axis_index("gz") > 0
    edge = [jnp.where(inside, edge[c], 0.0) for c in range(2)]

    def electric(z, h_below):
        curl = op.curl([h_new[c, z] for c in range(3)], h_below)
        store(z, curl, [base[c, z] for c in range(3)])

    electric(0, edge)

    def loop_e(z, carry):
        electric(z, [h_new[c, z - 1] for c in range(2)])
        return carry

    lax.fori_loop(1, planes, loop_e, 0)


def first_kernel(e_kz, h_kz, above, below, *refs):
    e_zk, h_zk, curl = refs[-3:]
    blocks, (ahead, h_new) = refs[:-5], refs[-5:-3]
    peers = len(blocks)
    me = lax.axis_index("mode")
    to_zk(e_kz, e_zk)
    to_zk(h_kz, h_zk)

    def store(z, found, base):
        for c in range(3):
            curl[c, z] = found[c]
            ahead[c, z] = base[c] + found[c]

    advance(peers, e_zk, e_zk, h_zk, above, below, h_new, store)
    planes = e_zk.shape[1] // peers
    for s in range(peers):
        first = peer(me, s, peers) * planes
        for c in range(2):
            for q in range(planes):
                blocks[s][c * planes + q] = curl[c, first + q]
        blocks[s][2 * planes] = curl[2, first]


def last_kernel(peers, e_zk, ahead, h_zk, above, below, ahead_new, h_kz, h_new):
    def store(z, found, base):
        for c in range(3):
            ahead_new[c, z] = base[c] + found[c]

    advance(peers, e_zk, ahead, h_zk, above, below, h_new, store)
    to_kz(h_new, h_kz)


def finish_kernel(ahead, *refs):
    blocks, (e_kz, e_zk, done, out_sem) = refs[:-4], refs[-4:]
    peers = len(blocks)
    planes = e_zk.shape[1] // peers
    stores = []
    for c in range(3):
        for s in range(peers):
            first = peer(lax.axis_index("mode"), s, peers) * planes
            for q in range(planes):
                e_zk[c, first + q] = ahead[c, first + q] - blocks[s][c * planes + q]
        to_kz(e_zk.at[pl.ds(c, 1)], done.at[pl.ds(c, 1)])
        stores.append(pltpu.make_async_copy(done.at[c], e_kz.at[c], out_sem.at[c]))
        stores[-1].start()
    for copy in stores:
        copy.wait()


def respond(table, fields, points, polar, velocity, coefficient, new_polar, new_velocity, store, q, base):
    high, low = table
    rows, angles = points.shape[1:]
    for c in range(3):
        f_high, f_low = split(fields(c).T)
        points[c] = (
            jnp.dot(f_high, high[...], preferred_element_type=jnp.float32)
            + jnp.dot(f_high, low[...], preferred_element_type=jnp.float32)
            + jnp.dot(f_low, high[...], preferred_element_type=jnp.float32)
        )
    width = min(angles, 256)

    def loop(g, carry):
        at = pl.ds(pl.multiple_of(g * 8, 8), 8)
        there = pl.ds(pl.multiple_of(base + g * 8, 8), 8)
        keep, push, spring, hard = [
            jnp.broadcast_to(coefficient[q, there, n : n + 1], (8, width)) for n in range(4)
        ]
        for start in range(0, angles, width):
            part = slice(start, start + width)
            before = [polar[c, 0, q, there, part] for c in range(3)]
            v = [velocity[c, 0, q, there, part] for c in range(3)]
            drive = [push * points[c, at, part] for c in range(3)]
            p = before
            for _ in range(SUBSTEPS):
                energy = p[0] * p[0] + p[1] * p[1] + p[2] * p[2]
                pull = spring + hard * energy
                v = [keep * v[c] + (drive[c] - pull * p[c]) for c in range(3)]
                p = [p[c] + v[c] for c in range(3)]
            for c in range(3):
                new_polar[c, 0, q, there, part] = p[c]
                new_velocity[c, 0, q, there, part] = v[c]
                points[c, at, part] = p[c] - before[c]
        return carry

    lax.fori_loop(0, rows // 8, loop, 0, unroll=2)
    modes = high.shape[0]
    weight = jnp.where(
        lax.broadcasted_iota(jnp.int32, (modes, rows), 0) == 0, 1.0 / angles, 2.0 / angles
    )
    contract = (((1,), (1,)), ((), ()))
    for c in range(3):
        c_high, c_low = split(points[c])
        modal = (
            lax.dot_general(high[...], c_high, contract, preferred_element_type=jnp.float32)
            + lax.dot_general(low[...], c_high, contract, preferred_element_type=jnp.float32)
            + lax.dot_general(high[...], c_low, contract, preferred_element_type=jnp.float32)
        )
        store(c, weight * modal)


def gas_step(fields, points, high, low, polar, velocity, coefficient, new_polar, new_velocity, change):
    planes = coefficient.shape[0]
    rows = points.shape[1]
    parts = coefficient.shape[1] // rows

    def chunk(n, carry):
        q, base = n // parts, pl.multiple_of(n % parts * rows, rows)
        at = pl.ds(base, rows)

        def store(c, modal):
            change[c * planes + q, :, at] = modal

        respond(
            (high, low), lambda c: fields[c * planes + q, :, at], points,
            polar, velocity, coefficient, new_polar, new_velocity, store, q, base,
        )
        return carry

    lax.fori_loop(0, planes * parts, chunk, 0)


def gas_first_kernel(peers, planes, basis, coefficient, polar, velocity, *refs):
    arrived, refs = refs[:peers], refs[peers:]
    blocks, refs = refs[:peers], refs[peers:]
    new_polar, new_velocity, change, rest, fields, points, high, low = refs
    me = lax.axis_index("mode")
    modes, radii = arrived[0].shape[1:]

    high[...], low[...] = split(basis[...])
    for s in range(peers):
        at = pl.ds(pl.multiple_of(peer(me, s, peers) * modes, modes), modes)
        for n in range(3 * planes):
            fields[n, at, :] = arrived[s][n]

    gas_step(fields, points, high, low, polar, velocity, coefficient, new_polar, new_velocity, change)

    for s in range(peers):
        first = peer(me, s, peers) * modes
        at = pl.ds(pl.multiple_of(first, modes), modes)
        op = Plane(first, modes, radii, modes * peers)
        for n in range(3 * planes):
            rest[n, at, :] = fields[n, at, :] - change[n, at, :]
        phi, axial = None, change[2 * planes, at, :]
        for q in range(planes):
            for c in range(2):
                sent = change[c * planes + q, at, :]
                if phi is not None:
                    sent = sent + (op.down(phi) if c == 0 else op.per_outer * op.rotate(phi))
                blocks[s][c * planes + q] = sent
            if q < planes - 1:
                phi = (-op.time_step / RATIO) * axial
                axial = axial + change[2 * planes + q + 1, at, :]
        blocks[s][2 * planes] = axial


def gas_last_kernel(peers, planes, basis, coefficient, polar, velocity, rest, earlier, *refs):
    arrived, refs = refs[:peers], refs[peers:]
    blocks, refs = refs[:peers], refs[peers:]
    new_polar, new_velocity, fields, points, change, high, low = refs
    me = lax.axis_index("mode")
    modes, radii = arrived[0].shape[1:]

    high[...], low[...] = split(basis[...])
    for s in range(peers):
        first = peer(me, s, peers) * modes
        at = pl.ds(pl.multiple_of(first, modes), modes)
        op = Plane(first, modes, radii, modes * peers)
        axial = arrived[s][2 * planes]
        for q in range(planes):
            radial, azimuth = arrived[s][q], arrived[s][planes + q]
            if q > 0:
                flux = op.up(op.inner * radial) + op.rotate(azimuth)
                axial = axial - (op.time_step / RATIO) * op.per_outer * flux
            for c, found in enumerate((radial, azimuth, axial)):
                n = c * planes + q
                fields[n, at, :] = rest[n, at, :] + found

    gas_step(fields, points, high, low, polar, velocity, coefficient, new_polar, new_velocity, change)

    for s in range(peers):
        at = pl.ds(pl.multiple_of(peer(me, s, peers) * modes, modes), modes)
        for n in range(3 * planes):
            blocks[s][n] = earlier[n, at, :] + change[n, at, :]


def f32(*shape):
    return jax.ShapeDtypeStruct(shape, jnp.float32)


def grant(*sizes):
    return pltpu.CompilerParams(vmem_limit_bytes=sum(sizes) * 5 // 4 + (1 << 20))


def nbytes(x):
    return 4 * math.prod(x if isinstance(x, tuple) else x.shape)


def call(kernel, out, *operands, scratch=(), tables=(), semaphores=(), flops=0, reads=pltpu.VMEM, writes=pltpu.VMEM, room=True):
    moved = sum(4 * math.prod(x.shape) for x in (*operands, *out))
    return pl.pallas_call(
        kernel,
        out_shape=out,
        in_specs=[pl.BlockSpec(memory_space=reads)] * len(operands),
        out_specs=[pl.BlockSpec(memory_space=writes)] * len(out),
        scratch_shapes=[pltpu.VMEM(shape, jnp.float32) for shape in scratch]
        + [pltpu.VMEM(shape, jnp.bfloat16) for shape in tables]
        + [pltpu.SemaphoreType.DMA(shape) for shape in semaphores],
        cost_estimate=pl.CostEstimate(flops=flops, bytes_accessed=moved, transcendentals=0),
        compiler_params=grant(*map(nbytes, (*operands, *out, *scratch, *tables))) if room else None,
    )(*operands)


def gas_call(kernel, basis, coefficient, polar, velocity, extra, arrived, blocks, kept, planes):
    modes, angles = basis.shape
    radii = polar.shape[3]
    rows = min(radii, LANES)
    held = (3 * planes, modes, radii)
    return call(
        functools.partial(kernel, len(arrived), planes),
        [*blocks, f32(*polar.shape), f32(*velocity.shape), *kept],
        basis, coefficient, polar, velocity, *extra, *arrived,
        scratch=[held, (3, rows, angles)] + ([] if kept else [held]), tables=[(modes, angles)] * 2,
        flops=12 * 3 * planes * radii * modes * angles,
    )


def exchange(blocks):
    peers = len(blocks)
    moved = []
    for s in range(peers - 1):
        inner, outer = (by_class[s] for by_class in distances(peers))
        pairs = [(i, i ^ (inner if is_inner(i, peers) else outer)) for i in range(peers)]
        moved.append(lax.ppermute(blocks[s], "mode", pairs))
    return moved + blocks[-1:]


def along(value, steps):
    count = lax.axis_size("gz")
    first, last = max(0, -steps), min(count, count - steps)
    return lax.ppermute(value, "gz", [(i, i + steps) for i in range(first, last)])


def run(efield, hfield, polar, velocity, material):
    peers = lax.axis_size("mode")
    _, modes, depth, radii = efield.shape
    planes = depth // peers
    angles = polar.shape[4]
    electric = [f32(3 * planes, modes, radii)] * peers
    curled = [f32(2 * planes + 1, modes, radii)] * peers
    zk = f32(3, depth, modes, radii)
    kz = f32(3, modes, depth, radii)
    lower, upper = f32(3, modes, radii), f32(2, 3, modes, radii)

    *blocks, to_lower, to_upper = call(
        pack_kernel, [*electric, lower, upper], efield, hfield,
        scratch=[kz.shape, zk.shape, (3, modes, 8, radii), lower.shape],
        semaphores=[(4,), (3, peers), (3,)], reads=pl.ANY, writes=pl.ANY, room=False,
    )
    arrived = exchange(blocks)
    above, below = along(to_lower, -1), along(to_upper, 1)

    stiff, damp, couple, harden = [material[n, 0] for n in range(4)]
    scale = 1.0 / (1.0 + 0.5 * damp)
    coefficient = jnp.stack(
        [(1.0 - 0.5 * damp) * scale, stiff * couple * scale, stiff * scale, 0.1 * harden * scale], axis=-1
    )
    basis = tables(modes * peers, angles)

    *curl_blocks, ahead, h_zk = call(
        first_kernel, [*curled, zk, zk], efield, hfield, above, below,
        scratch=[zk.shape, zk.shape, zk.shape],
    )
    curl_arrived = exchange(curl_blocks)

    held = f32(3 * planes, modes * peers, radii)
    *back, polar, velocity, change, rest = gas_call(
        gas_first_kernel, basis, coefficient, polar, velocity,
        [], arrived, curled, [held, held], planes,
    )
    returned = exchange(back)
    *back, polar, velocity = gas_call(
        gas_last_kernel, basis, coefficient, polar, velocity,
        [rest, change], curl_arrived, electric, [], planes,
    )
    total = exchange(back)

    e_zk, to_lower, to_upper = call(unpack_kernel, [zk, lower, upper], ahead, h_zk, *returned)
    above, below = along(to_lower, -1), along(to_upper, 1)
    ahead, new_hfield = call(
        functools.partial(last_kernel, peers), [zk, kz], e_zk, ahead, h_zk, above, below, scratch=[zk.shape]
    )
    (new_efield,) = call(
        finish_kernel, [kz], ahead, *total,
        scratch=[zk.shape, kz.shape], semaphores=[(3,)], writes=pltpu.HBM,
    )
    return new_efield, new_hfield, polar, velocity


def solution(mesh):
    field = P(None, "mode", "gz", None)
    state = P(None, "gz", "mode", None, None)
    return jax.shard_map(
        run,
        mesh=mesh,
        in_specs=(field, field, state, state, P(None, "gz", "mode", None)),
        out_specs=(field, field, state, state),
        check_vma=False,
    )
```

```python
import functools
import math

import jax
import jax.numpy as jnp
from jax import lax
from jax.experimental import pallas as pl
from jax.experimental.pallas import tpu as pltpu
from jax.sharding import PartitionSpec as P


SUBSTEPS = 4
LANES = 256
RATIO = 0.5


def distances(peers):
    quarter = peers // 4
    far, near = list(range(peers - 1, 3 * quarter - 1, -1)), list(range(1, quarter))
    middle = [s + odd for s in range(3 * quarter - 2, quarter - 1, -2) for odd in (0, 1)]
    inner, outer = far + near, near[:1] + far[1:] + far[:1] + near[1:]
    return inner + middle + [0], outer + middle + [0]


def is_even(s, peers):
    return distances(peers)[0][s] % 2 == 0


def evens(blocks):
    return [block for s, block in enumerate(blocks) if is_even(s, len(blocks))]


def of_pair(index, modes):
    return pl.ds(pl.multiple_of((index >> 1) * modes, modes), modes)


def peer(me, s, peers):
    inner, outer = (by_class[s] for by_class in distances(peers))
    if inner == outer:
        return me ^ inner
    return me ^ jnp.where(is_inner(me, peers), inner, outer)


def is_inner(me, peers):
    quarter = peers // 4
    return (me >= quarter) & (me < 3 * quarter)


def tables(modes, angles):
    order = jnp.arange(modes, dtype=jnp.int32) // 2
    parity = jnp.arange(modes, dtype=jnp.int32) % 2
    steps = jnp.arange(angles, dtype=jnp.int32)
    phase = order[:, None] * steps[None, :] % angles
    theta = phase.astype(jnp.float32) * (2.0 * math.pi / angles)
    return jnp.where(parity[:, None] == 0, jnp.cos(theta), jnp.sin(theta))


def split(value):
    high = value.astype(jnp.bfloat16)
    return high, (value - high.astype(jnp.float32)).astype(jnp.bfloat16)


class Plane:
    def __init__(self, first, modes, radii, total):
        row = lax.broadcasted_iota(jnp.int32, (modes, radii), 0)
        self.lane = lax.broadcasted_iota(jnp.int32, (modes, radii), 1)
        self.even = row % 2 == 0
        order = ((first + row) // 2).astype(jnp.float32)
        self.signed = jnp.where(self.even, order, -order)
        self.modes, self.radii = modes, radii
        self.time_step = 0.7 / total
        place = self.lane.astype(jnp.float32)
        self.outer = place + 1.0
        self.inner = place + 0.5
        self.per_outer = 1.0 / self.outer
        self.per_inner = 1.0 / self.inner

    def rotate(self, x):
        swapped = jnp.where(
            self.even, pltpu.roll(x, self.modes - 1, 0), pltpu.roll(x, 1, 0)
        )
        return self.signed * swapped

    def down(self, x):
        return x - jnp.where(self.lane == 0, 0.0, pltpu.roll(x, 1, 1))

    def up(self, x):
        return jnp.where(self.lane == self.radii - 1, 0.0, pltpu.roll(x, self.radii - 1, 1)) - x

    def flux(self, radial, azimuth):
        spread = self.up(self.inner * radial) + self.rotate(azimuth)
        return (self.time_step / RATIO) * self.per_outer * spread

    def magnetic(self, e, e_above, h):
        ts = self.time_step
        return (
            h[0] - (ts * self.per_outer) * self.rotate(e[2]) + RATIO * (e_above[1] - e[1]),
            h[1] - RATIO * (e_above[0] - e[0]) + ts * self.down(e[2]),
            h[2] - (ts * self.per_inner) * (self.down(self.outer * e[1]) - self.rotate(e[0])),
        )

    def curl(self, h, h_below):
        ts = self.time_step
        return (
            (ts * self.per_inner) * self.rotate(h[2]) - RATIO * (h[1] - h_below[1]),
            RATIO * (h[0] - h_below[0]) - ts * self.up(h[2]),
            (ts * self.per_outer) * (self.up(self.inner * h[1]) - self.rotate(h[0])),
        )


def to_zk(source, target):
    count, modes, planes, _ = source.shape
    for c in range(count):
        for k in range(0, modes, 8):
            for z in range(0, planes, 8):
                target[c, z : z + 8, k : k + 8, :] = jnp.swapaxes(
                    source[c, k : k + 8, z : z + 8, :], 0, 1
                )


def to_kz(source, target):
    count, planes, modes, _ = source.shape
    for c in range(count):
        for k in range(0, modes, 8):
            for z in range(0, planes, 8):
                target[c, k : k + 8, z : z + 8, :] = jnp.swapaxes(
                    source[c, z : z + 8, k : k + 8, :], 0, 1
                )


def pack_kernel(e_kz, h_kz, *refs):
    outs, (held, e_zk, tail, h_last, in_sem, out_sem, edge_sem) = refs[:-7], refs[-7:]
    blocks, (to_lower, to_upper) = outs[:-2], outs[-2:]
    peers = len(blocks)
    depth = e_zk.shape[1]
    planes = depth // peers
    me = lax.axis_index("mode")
    loads = [pltpu.make_async_copy(e_kz.at[c], held.at[c], in_sem.at[c]) for c in range(3)]
    loads.append(pltpu.make_async_copy(h_kz.at[:, :, pl.ds(depth - 8, 8)], tail, in_sem.at[3]))
    for load in loads:
        load.start()
    stores = []

    def store(source, target, semaphore):
        stores.append(pltpu.make_async_copy(source, target, semaphore))
        stores[-1].start()

    for c in range(3):
        loads[c].wait()
        to_zk(held.at[pl.ds(c, 1)], e_zk.at[pl.ds(c, 1)])
        for s in range(peers):
            first = peer(me, s, peers) * planes
            store(
                e_zk.at[c, pl.ds(first, planes)], blocks[s].at[pl.ds(c * planes, planes)], out_sem.at[c, s]
            )
    store(e_zk.at[:, 0], to_lower, edge_sem.at[0])
    store(e_zk.at[:, depth - 1], to_upper.at[0], edge_sem.at[1])
    loads[3].wait()
    for c in range(3):
        h_last[c] = tail[c, :, 7, :]
    store(h_last, to_upper.at[1], edge_sem.at[2])
    for copy in stores:
        copy.wait()


def unpack_kernel(ahead, h_zk, *refs):
    blocks, (e_zk, to_lower, to_upper) = refs[:-3], refs[-3:]
    peers = len(blocks)
    me = lax.axis_index("mode")
    planes = e_zk.shape[1] // peers
    last = e_zk.shape[1] - 1
    for s in range(peers):
        first = peer(me, s, peers) * planes
        for c in range(2):
            for q in range(planes):
                e_zk[c, first + q] = ahead[c, first + q] - blocks[s][c * planes + q]
        for q in range(planes):
            e_zk[2, first + q] = ahead[2, first + q]
    for s in range(peers):
        if is_even(s, peers):
            index = peer(me, s, peers)
            at = (index - (index & 1)) * planes + planes - 1
            e_zk[2, at] = ahead[2, at] - blocks[s][2 * planes]
    for c in range(3):
        to_lower[c] = e_zk[c, 0]
        to_upper[0, c] = e_zk[c, last]
        to_upper[1, c] = h_zk[c, last]


def advance(peers, e, base, h, above, below, h_new, store):
    planes, modes, radii = e.shape[1:]
    op = Plane(lax.axis_index("mode") * modes, modes, radii, modes * peers)

    def magnetic(z, e_above):
        new = op.magnetic([e[c, z] for c in range(3)], e_above, [h[c, z] for c in range(3)])
        for c in range(3):
            h_new[c, z] = new[c]

    def loop_h(z, carry):
        magnetic(z, [e[c, z + 1] for c in range(2)])
        return carry

    lax.fori_loop(0, planes - 1, loop_h, 0)
    magnetic(planes - 1, [above[c] for c in range(2)])
    edge = op.magnetic(
        [below[0, c] for c in range(3)], [e[c, 0] for c in range(2)], [below[1, c] for c in range(3)]
    )
    inside = lax.axis_index("gz") > 0
    edge = [jnp.where(inside, edge[c], 0.0) for c in range(2)]

    def electric(z, h_below):
        curl = op.curl([h_new[c, z] for c in range(3)], h_below)
        store(z, curl, [base[c, z] for c in range(3)])

    electric(0, edge)

    def loop_e(z, carry):
        electric(z, [h_new[c, z - 1] for c in range(2)])
        return carry

    lax.fori_loop(1, planes, loop_e, 0)


def first_kernel(e_kz, h_kz, above, below, *refs):
    e_zk, h_zk, curl = refs[-3:]
    blocks, (ahead, h_new) = refs[:-5], refs[-5:-3]
    peers = len(blocks)
    me = lax.axis_index("mode")
    to_zk(e_kz, e_zk)
    to_zk(h_kz, h_zk)

    def store(z, found, base):
        for c in range(3):
            curl[c, z] = found[c]
            ahead[c, z] = base[c] + found[c]

    advance(peers, e_zk, e_zk, h_zk, above, below, h_new, store)
    planes = e_zk.shape[1] // peers
    for s in range(peers):
        first = peer(me, s, peers) * planes
        for c in range(2):
            for q in range(planes):
                blocks[s][c * planes + q] = curl[c, first + q]
        if is_even(s, peers):
            blocks[s][2 * planes] = curl[2, first + (me & 1) * (planes - 1)]


def last_kernel(peers, e_zk, ahead, h_zk, above, below, ahead_new, h_kz, h_new):
    def store(z, found, base):
        for c in range(3):
            ahead_new[c, z] = base[c] + found[c]

    advance(peers, e_zk, ahead, h_zk, above, below, h_new, store)
    to_kz(h_new, h_kz)


def finish_kernel(ahead, *refs):
    blocks, (e_kz, e_zk, done, out_sem) = refs[:-4], refs[-4:]
    peers = len(blocks)
    planes = e_zk.shape[1] // peers
    stores = []
    for c in range(3):
        for s in range(peers):
            first = peer(lax.axis_index("mode"), s, peers) * planes
            for q in range(planes):
                e_zk[c, first + q] = ahead[c, first + q] - blocks[s][c * planes + q]
        to_kz(e_zk.at[pl.ds(c, 1)], done.at[pl.ds(c, 1)])
        stores.append(pltpu.make_async_copy(done.at[c], e_kz.at[c], out_sem.at[c]))
        stores[-1].start()
    for copy in stores:
        copy.wait()


def respond(table, fields, points, polar, velocity, coefficient, new_polar, new_velocity, store, q, base):
    high, low = table
    rows, angles = points.shape[1:]
    for c in range(3):
        f_high, f_low = split(fields(c).T)
        points[c] = (
            jnp.dot(f_high, high[...], preferred_element_type=jnp.float32)
            + jnp.dot(f_high, low[...], preferred_element_type=jnp.float32)
            + jnp.dot(f_low, high[...], preferred_element_type=jnp.float32)
        )
    width = min(angles, 256)

    def loop(g, carry):
        at = pl.ds(pl.multiple_of(g * 8, 8), 8)
        there = pl.ds(pl.multiple_of(base + g * 8, 8), 8)
        keep, push, spring, hard = [
            jnp.broadcast_to(coefficient[q, there, n : n + 1], (8, width)) for n in range(4)
        ]
        for start in range(0, angles, width):
            part = slice(start, start + width)
            before = [polar[c, 0, q, there, part] for c in range(3)]
            v = [velocity[c, 0, q, there, part] for c in range(3)]
            drive = [push * points[c, at, part] for c in range(3)]
            p = before
            for _ in range(SUBSTEPS):
                energy = p[0] * p[0] + p[1] * p[1] + p[2] * p[2]
                pull = spring + hard * energy
                v = [keep * v[c] + (drive[c] - pull * p[c]) for c in range(3)]
                p = [p[c] + v[c] for c in range(3)]
            for c in range(3):
                new_polar[c, 0, q, there, part] = p[c]
                new_velocity[c, 0, q, there, part] = v[c]
                points[c, at, part] = p[c] - before[c]
        return carry

    lax.fori_loop(0, rows // 8, loop, 0, unroll=4)
    modes = high.shape[0]
    weight = jnp.where(
        lax.broadcasted_iota(jnp.int32, (modes, rows), 0) == 0, 1.0 / angles, 2.0 / angles
    )
    contract = (((1,), (1,)), ((), ()))
    for c in range(3):
        c_high, c_low = split(points[c])
        modal = (
            lax.dot_general(high[...], c_high, contract, preferred_element_type=jnp.float32)
            + lax.dot_general(low[...], c_high, contract, preferred_element_type=jnp.float32)
            + lax.dot_general(high[...], c_low, contract, preferred_element_type=jnp.float32)
        )
        store(c, weight * modal)


def gas_step(fields, points, high, low, polar, velocity, coefficient, new_polar, new_velocity, change):
    planes = coefficient.shape[0]
    rows = points.shape[1]
    parts = coefficient.shape[1] // rows

    def chunk(n, carry):
        q, base = n // parts, pl.multiple_of(n % parts * rows, rows)
        at = pl.ds(base, rows)

        def store(c, modal):
            change[c * planes + q, :, at] = modal

        respond(
            (high, low), lambda c: fields[c * planes + q, :, at], points,
            polar, velocity, coefficient, new_polar, new_velocity, store, q, base,
        )
        return carry

    lax.fori_loop(0, planes * parts, chunk, 0)


def gas_first_kernel(peers, planes, basis, coefficient, polar, velocity, *refs):
    arrived, refs = refs[:peers], refs[peers:]
    blocks, refs = refs[:peers], refs[peers:]
    new_polar, new_velocity, change, rest, message, fields, points, high, low = refs
    me = lax.axis_index("mode")
    modes, radii = arrived[0].shape[1:]

    high[...], low[...] = split(basis[...])
    for s in range(peers):
        at = pl.ds(pl.multiple_of(peer(me, s, peers) * modes, modes), modes)
        for n in range(3 * planes):
            fields[n, at, :] = arrived[s][n]

    gas_step(fields, points, high, low, polar, velocity, coefficient, new_polar, new_velocity, change)

    for s in range(peers):
        index = peer(me, s, peers)
        at = pl.ds(pl.multiple_of(index * modes, modes), modes)
        op = Plane(index * modes, modes, radii, modes * peers)
        for n in range(3 * planes):
            rest[n, at, :] = fields[n, at, :] - change[n, at, :]
        total = change[2 * planes, at, :]
        for q in range(1, planes):
            total = total + change[2 * planes + q, at, :]
        if is_even(s, peers):
            blocks[s][2 * planes] = total
        else:
            message[of_pair(index, modes)] = total
        below = jnp.where(me % 2 == 1, total, 0.0)
        for q in range(planes):
            phi = (op.time_step / RATIO) * below
            blocks[s][q] = change[q, at, :] + op.down(phi)
            blocks[s][planes + q] = change[planes + q, at, :] + op.per_outer * op.rotate(phi)
            below = below - change[2 * planes + q, at, :]


def seal_kernel(peers, message, *refs):
    blocks, sealed = refs[: len(refs) // 2], refs[len(refs) // 2 :]
    me = lax.axis_index("mode")
    where = [s for s in range(peers) if is_even(s, peers)]
    for s, block, out in zip(where, blocks, sealed):
        count, modes, _ = block.shape
        for n in range(count - 1):
            out[n] = block[n]
        out[count - 1] = block[count - 1] + message[of_pair(peer(me, s, peers), modes)]


def recover_kernel(peers, *refs):
    blocks, message = refs[:-1], refs[-1]
    me = lax.axis_index("mode")
    where = [s for s in range(peers) if is_even(s, peers)]
    for s, block in zip(where, blocks):
        count, modes, radii = block.shape
        planes = count // 2
        index = peer(me, s, peers)
        op = Plane(index * modes, modes, radii, modes * peers)
        flux = [op.flux(block[q], block[planes + q]) for q in range(planes)]
        first = block[2 * planes]
        message[of_pair(index, modes)] = jnp.where(me % 2 == 1, first + sum(flux), first - sum(flux[1:]))


def gas_last_kernel(peers, planes, basis, coefficient, polar, velocity, rest, earlier, message, *refs):
    arrived, refs = refs[:peers], refs[peers:]
    blocks, refs = refs[:peers], refs[peers:]
    new_polar, new_velocity, fields, points, change, high, low = refs
    me = lax.axis_index("mode")
    modes, radii = arrived[0].shape[1:]

    high[...], low[...] = split(basis[...])
    for s in range(peers):
        index = peer(me, s, peers)
        at = pl.ds(pl.multiple_of(index * modes, modes), modes)
        op = Plane(index * modes, modes, radii, modes * peers)
        flux = [op.flux(arrived[s][q], arrived[s][planes + q]) for q in range(planes)]
        if is_even(s, peers):
            known = arrived[s][2 * planes]
            axial = known + jnp.where(me % 2 == 1, sum(flux[1:]), 0.0)
        else:
            known = message[of_pair(index, modes)]
            axial = known + jnp.where(me % 2 == 1, -flux[0], sum(flux[1:]))
        for q in range(planes):
            if q > 0:
                axial = axial - flux[q]
            for c, found in enumerate((arrived[s][q], arrived[s][planes + q], axial)):
                n = c * planes + q
                fields[n, at, :] = rest[n, at, :] + found

    gas_step(fields, points, high, low, polar, velocity, coefficient, new_polar, new_velocity, change)

    for s in range(peers):
        at = pl.ds(pl.multiple_of(peer(me, s, peers) * modes, modes), modes)
        for n in range(3 * planes):
            blocks[s][n] = earlier[n, at, :] + change[n, at, :]


def f32(*shape):
    return jax.ShapeDtypeStruct(shape, jnp.float32)


def grant(*sizes):
    return pltpu.CompilerParams(vmem_limit_bytes=sum(sizes) * 5 // 4 + (1 << 20))


def nbytes(x):
    return 4 * math.prod(x if isinstance(x, tuple) else x.shape)


def call(kernel, out, *operands, scratch=(), tables=(), semaphores=(), flops=0, reads=pltpu.VMEM, writes=pltpu.VMEM, room=True):
    moved = sum(4 * math.prod(x.shape) for x in (*operands, *out))
    return pl.pallas_call(
        kernel,
        out_shape=out,
        in_specs=[pl.BlockSpec(memory_space=reads)] * len(operands),
        out_specs=[pl.BlockSpec(memory_space=writes)] * len(out),
        scratch_shapes=[pltpu.VMEM(shape, jnp.float32) for shape in scratch]
        + [pltpu.VMEM(shape, jnp.bfloat16) for shape in tables]
        + [pltpu.SemaphoreType.DMA(shape) for shape in semaphores],
        cost_estimate=pl.CostEstimate(flops=flops, bytes_accessed=moved, transcendentals=0),
        compiler_params=grant(*map(nbytes, (*operands, *out, *scratch, *tables))) if room else None,
    )(*operands)


def gas_call(kernel, basis, coefficient, polar, velocity, extra, arrived, blocks, kept, planes):
    modes, angles = basis.shape
    radii = polar.shape[3]
    rows = min(radii, LANES)
    held = (3 * planes, modes, radii)
    return call(
        functools.partial(kernel, len(arrived), planes),
        [*blocks, f32(*polar.shape), f32(*velocity.shape), *kept],
        basis, coefficient, polar, velocity, *extra, *arrived,
        scratch=[held, (3, rows, angles)] + ([] if kept else [held]), tables=[(modes, angles)] * 2,
        flops=12 * 3 * planes * radii * modes * angles,
    )


def exchange(blocks):
    peers = len(blocks)
    moved = []
    for s in range(peers - 1):
        inner, outer = (by_class[s] for by_class in distances(peers))
        pairs = [(i, i ^ (inner if is_inner(i, peers) else outer)) for i in range(peers)]
        moved.append(lax.ppermute(blocks[s], "mode", pairs))
    return moved + blocks[-1:]


def along(value, steps):
    count = lax.axis_size("gz")
    first, last = max(0, -steps), min(count, count - steps)
    return lax.ppermute(value, "gz", [(i, i + steps) for i in range(first, last)])


def swap(value):
    return lax.ppermute(value, "mode", [(i, i ^ 1) for i in range(lax.axis_size("mode"))])


def run(efield, hfield, polar, velocity, material):
    peers = lax.axis_size("mode")
    _, modes, depth, radii = efield.shape
    planes = depth // peers
    angles = polar.shape[4]
    electric = [f32(3 * planes, modes, radii)] * peers
    curled = [f32(2 * planes + is_even(s, peers), modes, radii) for s in range(peers)]
    half = f32(modes * peers // 2, radii)
    zk = f32(3, depth, modes, radii)
    kz = f32(3, modes, depth, radii)
    lower, upper = f32(3, modes, radii), f32(2, 3, modes, radii)

    *blocks, to_lower, to_upper = call(
        pack_kernel, [*electric, lower, upper], efield, hfield,
        scratch=[kz.shape, zk.shape, (3, modes, 8, radii), lower.shape],
        semaphores=[(4,), (3, peers), (3,)], reads=pl.ANY, writes=pl.ANY, room=False,
    )
    arrived = exchange(blocks)
    above, below = along(to_lower, -1), along(to_upper, 1)

    stiff, damp, couple, harden = [material[n, 0] for n in range(4)]
    scale = 1.0 / (1.0 + 0.5 * damp)
    coefficient = jnp.stack(
        [(1.0 - 0.5 * damp) * scale, stiff * couple * scale, stiff * scale, 0.1 * harden * scale], axis=-1
    )
    basis = tables(modes * peers, angles)

    *curl_blocks, ahead, h_zk = call(
        first_kernel, [*curled, zk, zk], efield, hfield, above, below,
        scratch=[zk.shape, zk.shape, zk.shape],
    )
    curl_arrived = exchange(curl_blocks)

    held = f32(3 * planes, modes * peers, radii)
    *back, polar, velocity, change, rest, sums = gas_call(
        gas_first_kernel, basis, coefficient, polar, velocity,
        [], arrived, curled, [held, held, half], planes,
    )
    sealed = iter(call(functools.partial(seal_kernel, peers), evens(curled), swap(sums), *evens(back)))
    back = [next(sealed) if is_even(s, peers) else block for s, block in enumerate(back)]
    returned = exchange(back)
    (axial,) = call(functools.partial(recover_kernel, peers), [half], *evens(curl_arrived))
    axial = swap(axial)
    *back, polar, velocity = gas_call(
        gas_last_kernel, basis, coefficient, polar, velocity,
        [rest, change, axial], curl_arrived, electric, [], planes,
    )
    total = exchange(back)

    e_zk, to_lower, to_upper = call(unpack_kernel, [zk, lower, upper], ahead, h_zk, *returned)
    above, below = along(to_lower, -1), along(to_upper, 1)
    ahead, new_hfield = call(
        functools.partial(last_kernel, peers), [zk, kz], e_zk, ahead, h_zk, above, below, scratch=[zk.shape]
    )
    (new_efield,) = call(
        finish_kernel, [kz], ahead, *total,
        scratch=[zk.shape, kz.shape], semaphores=[(3,)], writes=pltpu.HBM,
    )
    return new_efield, new_hfield, polar, velocity


def solution(mesh):
    field = P(None, "mode", "gz", None)
    state = P(None, "gz", "mode", None, None)
    return jax.shard_map(
        run,
        mesh=mesh,
        in_specs=(field, field, state, state, P(None, "gz", "mode", None)),
        out_specs=(field, field, state, state),
        check_vma=False,
    )
```
